1024 devices in a mesh: ctx: 32 (over y, z_lo), pipe: 16 (over x, z_hi), dp: 2 (over core).
Axes of the slice: x: 4, y: 4, z: 32 (z_hi: 4, z_lo: 8; z = z_hi * 8 + z_lo), core: 2. Of those that a mesh axis runs over, the one named last changes fastest.
Arguments:
- queries: bfloat16 [16, 4096, 4096], P('pipe', 'ctx', 'dp'), may hold values from -128 to 128
- keys: bfloat16 [16, 4096, 512], P('pipe', 'ctx', 'dp'), may hold values from -6 to 6
- values: bfloat16 [16, 4096, 512], P('pipe', 'ctx', 'dp'), may hold values from -6 to 6
- out_grad: bfloat16 [16, 4096, 4096], P('pipe', 'ctx', 'dp'), may hold values from -6 to 6
- doc_lengths: int32 [16, 16], P('pipe'), may hold values from 1 to 512, 4096 in all within a row
Outputs:
- next_rows: bfloat16 [16, 4096, 4096], P('pipe', ('ctx', 'dp'))
- query_grad: bfloat16 [16, 4096, 4096], P('pipe', 'ctx', 'dp')
- key_gradient: bfloat16 [16, 4096, 512], P('pipe', 'ctx', 'dp')
- value_gradient: bfloat16 [16, 4096, 512], P('pipe', 'ctx', 'dp')
The draws below stay inside these ranges and needn't reach their ends.
Inputs may be any that keep to these rules, and one draw needn't show every extreme that they name: `doc_lengths`: each row sums to 4096; its longest document has exactly 512 positions.
All inputs are finite; a program needn't handle non-finite values.
Results may differ from the reference program's by a relative error of at most 0.04.
Values may be sent and summed in bfloat16 or wider, within the bound.
No kernel may reach another device: no remote copies, remote signals or barrier semaphores. Data moves between devices by JAX's collectives and lax.ppermute only.
A program may use at most 32 MiB of HBM per device.

```python
import math
import jax
import jax.numpy as jnp
import numpy as np
from jax import lax

QUERY_HEAD_COUNT = 32
KEY_VALUE_HEADS = 4
HEAD_SIZE = 128
TOK_DEV = 128
DEPTH = 4
MOST_DOC = 512
PACKED_LENGTH = 4096
DOCS = 16
CASCADE_SECTIONS = 16


def base_field(key):
    return jax.random.normal(jax.random.fold_in(key, 11), (CASCADE_SECTIONS, PACKED_LENGTH, KEY_VALUE_HEADS, HEAD_SIZE), jnp.float32)


def draw_keys(key, part):
    key_region = base_field(key)
    key_region = jnp.clip(key_region, -6.0, 6.0)
    return key_region.reshape(CASCADE_SECTIONS, PACKED_LENGTH, KEY_VALUE_HEADS * HEAD_SIZE).astype(jnp.bfloat16)


def draw_queries(key, part):
    query_field = jax.random.normal(jax.random.fold_in(key, 21), (CASCADE_SECTIONS, PACKED_LENGTH, QUERY_HEAD_COUNT, HEAD_SIZE), jnp.float32)
    query_field = jnp.clip(query_field, -128.0, 128.0)
    return query_field.reshape(CASCADE_SECTIONS, PACKED_LENGTH, QUERY_HEAD_COUNT * HEAD_SIZE).astype(jnp.bfloat16)


def block_levels(key, shape, cuts, low, high):
    def one(dim, parts):
        draws = jax.random.uniform(jax.random.fold_in(jax.random.fold_in(key, 6), dim), (parts,), jnp.float32, low / len(cuts), high / len(cuts))
        return jnp.repeat(jnp.exp(draws), shape[dim] // parts).reshape((-1,) + (1,) * (len(shape) - dim - 1))

    loudness = one(*cuts[0])
    for cut in cuts[1:]:
        loudness = loudness * one(*cut)
    return loudness


def length_profile(amount, total, bound, slope):
    weights = [(1 << 20) // math.isqrt(standing ** slope) + 1 for standing in range(2, amount + 1)]
    spare, holding = total - bound - (amount - 1), [1] * (amount - 1)
    while spare > 0:
        candidates = [i for i in range(amount - 1) if holding[i] < bound]
        whole, remaining = sum([weights[i] for i in candidates]), spare
        for i in candidates:
            more = min(bound - holding[i], max(1, remaining * weights[i] // whole), spare)
            holding[i] = holding[i] + more
            spare = spare - more
    return np.array([bound] + holding)


def uneven_parts(key, amount, total, bound, slope):
    if amount == 2:
        one = jax.random.randint(key, (), max(1, total - bound), min(bound, total - 1) + 1)
        return jnp.stack([one, total - one])
    sizes = jnp.asarray(length_profile(amount, total, bound, slope), jnp.int32)
    twos = (amount - 1) // 2
    donor, sink = sizes[1:1 + 2 * twos:2], sizes[2:2 + 2 * twos:2]
    margin = jnp.minimum(donor - 1, bound - sink)
    moved = jax.random.randint(jax.random.fold_in(key, 1), (twos,), 0, 1 << 20) % (margin + 1)
    sizes = sizes.at[1:1 + 2 * twos:2].set(donor - moved).at[2:2 + 2 * twos:2].set(sink + moved)
    return sizes[jax.random.permutation(jax.random.fold_in(key, 2), amount)]


def centred(key, shape, deviation, bound, cuts=(), held_as=jnp.bfloat16):
    entries = deviation * jax.random.normal(key, shape, jnp.float32)
    if cuts:
        entries = entries * block_levels(key, shape, cuts, -0.22, 0.18)
    return jnp.clip(entries, -bound, bound).astype(held_as)


def setup_inputs(seed: int = 0) -> dict:
    splits = jax.random.split(jax.random.key(seed), 6)
    queries = draw_queries(jax.random.fold_in(splits[5], 71), 0)
    keys = draw_keys(jax.random.fold_in(splits[5], 71), 0)
    values = centred(splits[2], (CASCADE_SECTIONS, PACKED_LENGTH, KEY_VALUE_HEADS * HEAD_SIZE), 1.0, 6.0, ((0, 16), (1, 32), (2, 2)))
    out_grad = centred(splits[3], (CASCADE_SECTIONS, PACKED_LENGTH, QUERY_HEAD_COUNT * HEAD_SIZE), 1.0, 6.0, ((0, 16), (1, 32), (2, 2)))
    doc_lengths = jax.vmap(lambda own: uneven_parts(own, DOCS, PACKED_LENGTH, MOST_DOC, 2))(jax.random.split(splits[4], CASCADE_SECTIONS)).reshape((CASCADE_SECTIONS, DOCS)).astype(jnp.int32)
    return dict(queries=queries, keys=keys, values=values, out_grad=out_grad, doc_lengths=doc_lengths)


def forward_head(query_head, key_head, value_head, positions, doc_ids):
    sequence_length = query_head.shape[0]
    block_count = sequence_length // TOK_DEV
    score_scale = HEAD_SIZE ** -0.5
    query_blocks = query_head.reshape(block_count, TOK_DEV, HEAD_SIZE).astype(jnp.float32)
    key_blocks = key_head.reshape(block_count, TOK_DEV, HEAD_SIZE)
    value_blocks = value_head.reshape(block_count, TOK_DEV, HEAD_SIZE)
    query_pos = positions.reshape(block_count, TOK_DEV)
    query_doc = doc_ids.reshape(block_count, TOK_DEV)
    run_max = jnp.full((block_count, TOK_DEV), -jnp.inf, jnp.float32)
    run_total = jnp.zeros((block_count, TOK_DEV), jnp.float32)
    run_sum = jnp.zeros((block_count, TOK_DEV, HEAD_SIZE), jnp.float32)
    for offset in range(DEPTH + 1):
        shifted_keys = jnp.concatenate([jnp.zeros((offset, TOK_DEV, HEAD_SIZE), key_blocks.dtype), key_blocks[:block_count - offset]], axis=0)
        shifted_values = jnp.concatenate([jnp.zeros((offset, TOK_DEV, HEAD_SIZE), value_blocks.dtype), value_blocks[:block_count - offset]], axis=0)
        key_pos = query_pos - offset * TOK_DEV
        key_doc = jnp.concatenate([jnp.full((offset, TOK_DEV), -1, jnp.int32), query_doc[:block_count - offset]], axis=0)
        allowed = (query_doc[:, :, None] == key_doc[:, None, :]) & (key_pos[:, None, :] <= query_pos[:, :, None]) & (key_pos[:, None, :] >= 0)
        scores = score_scale * jnp.einsum("btd,bud->btu", query_blocks, shifted_keys.astype(jnp.float32))
        scores = jnp.where(allowed, scores, -jnp.inf)
        new_max = jnp.maximum(run_max, jnp.max(scores, axis=2))
        safe_max = jnp.where(jnp.isfinite(new_max), new_max, 0.0)
        rescale = jnp.exp(run_max - safe_max)
        weights = jnp.exp(scores - safe_max[:, :, None])
        run_total = run_total * rescale + jnp.sum(weights, axis=2)
        weights_low = weights.astype(jnp.bfloat16)
        run_sum = run_sum * rescale[:, :, None] + jnp.einsum("btu,bud->btd", weights_low.astype(jnp.float32), shifted_values.astype(jnp.float32))
        run_max = new_max
    attended = (run_sum / run_total[:, :, None]).reshape(sequence_length, HEAD_SIZE).astype(jnp.bfloat16)
    log_total = (run_max + jnp.log(run_total)).reshape(sequence_length)
    return attended, log_total


def section_grads(queries, keys, values, out_grad, lengths):
    sequence_length = queries.shape[0]
    query_group_size = QUERY_HEAD_COUNT // KEY_VALUE_HEADS
    doc_ends = jnp.cumsum(lengths).astype(jnp.int32)
    positions = jnp.arange(sequence_length, dtype=jnp.int32)
    doc_ids = jnp.sum((positions[:, None] >= doc_ends[None, :]).astype(jnp.int32), axis=1)
    allowed = (doc_ids[:, None] == doc_ids[None, :]) & (positions[None, :] <= positions[:, None])
    query_heads = queries.reshape(sequence_length, QUERY_HEAD_COUNT, HEAD_SIZE).transpose(1, 0, 2)
    grad_heads = out_grad.reshape(sequence_length, QUERY_HEAD_COUNT, HEAD_SIZE).transpose(1, 0, 2)
    key_head_rows = keys.reshape(sequence_length, KEY_VALUE_HEADS, HEAD_SIZE).transpose(1, 0, 2)
    value_head_rows = values.reshape(sequence_length, KEY_VALUE_HEADS, HEAD_SIZE).transpose(1, 0, 2)
    score_scale = HEAD_SIZE ** -0.5

    def forward_one(head_index):
        return forward_head(query_heads[head_index], key_head_rows[head_index // query_group_size], value_head_rows[head_index // query_group_size], positions, doc_ids)

    attended_heads, log_totals = lax.map(forward_one, jnp.arange(QUERY_HEAD_COUNT, dtype=jnp.int32))

    def backward_one(head_index):
        query_block = query_heads[head_index]
        grad_block = grad_heads[head_index]
        key_block = key_head_rows[head_index // query_group_size]
        value_block = value_head_rows[head_index // query_group_size]
        attended = attended_heads[head_index]
        log_total = log_totals[head_index]
        scores = score_scale * jnp.dot(query_block, key_block.T, preferred_element_type=jnp.float32)
        scores = jnp.where(allowed, scores, -jnp.inf)
        probs = jnp.exp(scores - log_total[:, None])
        probs_low = probs.astype(jnp.bfloat16)
        row_delta = jnp.sum(grad_block.astype(jnp.float32) * attended.astype(jnp.float32), axis=1)
        prob_grad = jnp.dot(grad_block, value_block.T, preferred_element_type=jnp.float32)
        score_grad = (probs * (prob_grad - row_delta[:, None])).astype(jnp.bfloat16)
        query_grad = (score_scale * jnp.dot(score_grad, key_block, preferred_element_type=jnp.float32)).astype(jnp.bfloat16)
        key_portion = score_scale * jnp.dot(score_grad.T, query_block, preferred_element_type=jnp.float32)
        value_portion = jnp.dot(probs_low.T, grad_block, preferred_element_type=jnp.float32)
        return query_grad, key_portion, value_portion

    query_grad, key_portion, value_portion = lax.map(backward_one, jnp.arange(QUERY_HEAD_COUNT, dtype=jnp.int32))
    attended = attended_heads.transpose(1, 0, 2).reshape(sequence_length, QUERY_HEAD_COUNT * HEAD_SIZE)
    query_grad = query_grad.transpose(1, 0, 2).reshape(sequence_length, QUERY_HEAD_COUNT * HEAD_SIZE)
    key_gradient = key_portion.reshape(KEY_VALUE_HEADS, query_group_size, sequence_length, HEAD_SIZE).sum(axis=1).transpose(1, 0, 2).reshape(sequence_length, KEY_VALUE_HEADS * HEAD_SIZE).astype(jnp.bfloat16)
    value_gradient = value_portion.reshape(KEY_VALUE_HEADS, query_group_size, sequence_length, HEAD_SIZE).sum(axis=1).transpose(1, 0, 2).reshape(sequence_length, KEY_VALUE_HEADS * HEAD_SIZE).astype(jnp.bfloat16)
    return attended, query_grad, key_gradient, value_gradient


def section_tuple(operands):
    return section_grads(operands[0], operands[1], operands[2], operands[3], operands[4])


def reference(queries, keys, values, out_grad, doc_lengths):
    attended, query_grad, key_gradient, value_gradient = lax.map(section_tuple, (queries, keys, values, out_grad, doc_lengths))
    next_rows = jnp.roll(attended, 1, axis=0)
    return (next_rows, query_grad, key_gradient, value_gradient)
```

```python
import functools
import jax
import jax.numpy as jnp
from jax import lax
from jax.experimental import pallas as pl
from jax.experimental.pallas import tpu as pltpu
from jax.sharding import PartitionSpec as P

HEAD_SIZE = 128
REACH = 4
PAIR = 2


NT = (((1,), (1,)), ((), ()))
NN = (((1,), (0,)), ((), ()))


def dot(left, right, dims):
    return lax.dot_general(left, right, dims, preferred_element_type=jnp.float32)


def shifted(array, by):
    length = lax.axis_size("ctx")
    pairs = [(i, i + by) for i in range(length) if 0 <= i + by < length]
    return lax.ppermute(array, "ctx", pairs)


def to_next_section(array, cross):
    sections, cores = lax.axis_size("pipe"), lax.axis_size("dp")
    pairs = [
        (p * cores + d, ((p + 1) % sections) * cores + (d ^ cross))
        for p in range(sections)
        for d in range(cores)
    ]
    return lax.ppermute(array, ("pipe", "dp"), pairs)


def allowed_tile(where_ref, lengths_ref, rows, keys_seen):
    first = where_ref[0] * rows
    query_pos = first + lax.broadcasted_iota(jnp.int32, (1, rows), 1)
    start = jnp.zeros((1, rows), jnp.int32)
    end = jnp.int32(0)
    for i in range(lengths_ref.shape[1]):
        end = end + lengths_ref[0, i]
        start = jnp.where(query_pos >= end, end, start)
    key_pos = first - (keys_seen - rows) + lax.broadcasted_iota(jnp.int32, (keys_seen, rows), 0)
    bias = jnp.where((key_pos >= start) & (key_pos <= query_pos), 0.0, -jnp.inf)
    return jnp.concatenate([bias] * PAIR, axis=1)


def gathered(far_refs, own_ref, which, j):
    cols = slice(j * HEAD_SIZE, (j + 1) * HEAD_SIZE)
    return jnp.concatenate([r[which, :, cols] for r in far_refs] + [own_ref[:, cols]], axis=0)


def stacked(ref, g):
    return jnp.concatenate(
        [ref[:, h * HEAD_SIZE : (h + 1) * HEAD_SIZE] for h in range(PAIR * g, PAIR * (g + 1))], axis=0
    )


def turned(block):
    return jnp.transpose(block.astype(jnp.float32)).astype(jnp.bfloat16)


def forward_kernel(where_ref, lengths_ref, q_ref, k_ref, v_ref, f4, f3, f2, f1,
                   same_ref, other_ref, stats_ref, bias_ref, att_ref, *, groups):
    rows = q_ref.shape[0]
    far = (f4, f3, f2, f1)
    seen = rows * (REACH + 1)
    scale = HEAD_SIZE ** -0.5
    bias_ref[...] = allowed_tile(where_ref, lengths_ref, rows, seen)
    for j in range(k_ref.shape[1] // HEAD_SIZE):
        keys = gathered(far, k_ref, 0, j)
        values_t = turned(gathered(far, v_ref, 1, j))
        for g in range(j * groups // PAIR, (j + 1) * groups // PAIR):
            scores = dot(keys, stacked(q_ref, g), NT) + bias_ref[...]
            top = jnp.max(scores, axis=0, keepdims=True)
            weights = jnp.exp((scores - top) * scale)
            total = jnp.sum(weights, axis=0, keepdims=True)
            inverse = 1.0 / total
            sums = dot(values_t, weights.astype(jnp.bfloat16), NN) * inverse
            stats_ref[2 * g : 2 * g + 1, :] = top
            stats_ref[2 * g + 1 : 2 * g + 2, :] = inverse
            for i in range(PAIR):
                h = PAIR * g + i
                att_ref[:, h * HEAD_SIZE : (h + 1) * HEAD_SIZE] = jnp.transpose(
                    sums[:, i * rows : (i + 1) * rows]
                ).astype(jnp.bfloat16)
    half = rows // 2
    core = where_ref[1]
    same_ref[...] = att_ref[pl.ds(pl.multiple_of(core * half, half), half), :]
    other_ref[...] = att_ref[pl.ds(pl.multiple_of((1 - core) * half, half), half), :]


def backward_kernel(where_ref, lengths_ref, q_ref, g_ref, k_ref, v_ref, f4, f3, f2, f1, stats_ref,
                    dq_ref, o4, o3, o2, o1, own_ref, bias_ref, ds_ref, p_ref, *, groups):
    rows = q_ref.shape[0]
    far = (f4, f3, f2, f1)
    out = (o4, o3, o2, o1)
    seen = rows * (REACH + 1)
    scale = HEAD_SIZE ** -0.5
    wide = PAIR * rows
    bias_ref[...] = allowed_tile(where_ref, lengths_ref, rows, seen)
    for j in range(k_ref.shape[1] // HEAD_SIZE):
        keys = gathered(far, k_ref, 0, j)
        values = gathered(far, v_ref, 1, j)
        keys_t = turned(keys)
        for n in range(groups // PAIR):
            g = j * groups // PAIR + n
            top = stats_ref[2 * g : 2 * g + 1, :]
            inverse = stats_ref[2 * g + 1 : 2 * g + 2, :]
            scores = dot(keys, stacked(q_ref, g), NT) + bias_ref[...]
            probs = jnp.exp((scores - top) * scale) * inverse
            p_ref[:, n * wide : (n + 1) * wide] = probs.astype(jnp.bfloat16)
            prob_grad = dot(values, stacked(g_ref, g), NT)
            delta = jnp.sum(probs * prob_grad, axis=0, keepdims=True)
            score_grad = (probs * (prob_grad - delta)).astype(jnp.bfloat16)
            ds_ref[:, n * wide : (n + 1) * wide] = score_grad
            sums = dot(keys_t, score_grad, NN) * scale
            for i in range(PAIR):
                h = PAIR * g + i
                dq_ref[:, h * HEAD_SIZE : (h + 1) * HEAD_SIZE] = jnp.transpose(
                    sums[:, i * rows : (i + 1) * rows]
                ).astype(jnp.bfloat16)
        cols = slice(j * HEAD_SIZE, (j + 1) * HEAD_SIZE)
        rank = range(j * groups // PAIR, (j + 1) * groups // PAIR)
        q_all = jnp.concatenate([stacked(q_ref, g) for g in rank], axis=0)
        g_all = jnp.concatenate([stacked(g_ref, g) for g in rank], axis=0)
        key_part = dot(ds_ref[...], q_all, NN) * scale
        value_part = dot(p_ref[...], g_all, NN)
        for n, ref in enumerate(out + (own_ref,)):
            ref[0, :, cols] = key_part[n * rows : (n + 1) * rows, :].astype(ref.dtype)
            ref[1, :, cols] = value_part[n * rows : (n + 1) * rows, :].astype(ref.dtype)


def per_device(queries, keys, values, out_grad, doc_lengths):
    rows, width = queries.shape[1:]
    kv_width = keys.shape[2]
    groups = width // kv_width
    seen = rows * (REACH + 1)
    queries, keys, values, out_grad = queries[0], keys[0], values[0], out_grad[0]
    core = lax.axis_index("dp")
    where = jnp.stack([lax.axis_index("ctx"), core]).astype(jnp.int32)
    kv_pair = jnp.stack([keys, values])
    far = [shifted(kv_pair, by) for by in range(REACH, 0, -1)]

    smem = pl.BlockSpec(memory_space=pltpu.SMEM)
    vmem = pl.BlockSpec(memory_space=pltpu.VMEM)
    pair_count = width // HEAD_SIZE // PAIR
    wide = PAIR * rows
    half = jax.ShapeDtypeStruct((rows // 2, width), jnp.bfloat16)
    same, other, stats = pl.pallas_call(
        functools.partial(forward_kernel, groups=groups),
        out_shape=(half, half, jax.ShapeDtypeStruct((2 * pair_count, wide), jnp.float32)),
        in_specs=[smem, smem] + [vmem] * 7,
        out_specs=(vmem,) * 3,
        scratch_shapes=[
            pltpu.VMEM((seen, wide), jnp.float32),
            pltpu.VMEM((rows, width), jnp.bfloat16),
        ],
        name="attend",
    )(where, doc_lengths, queries, keys, values, *far)
    same = to_next_section(same, 0)
    other = to_next_section(other, 1)

    moved = jax.ShapeDtypeStruct((2, rows, kv_width), jnp.bfloat16)
    query_grad, *parts, own = pl.pallas_call(
        functools.partial(backward_kernel, groups=groups),
        out_shape=(jax.ShapeDtypeStruct((rows, width), jnp.bfloat16),)
        + (moved,) * REACH
        + (jax.ShapeDtypeStruct((2, rows, kv_width), jnp.float32),),
        in_specs=[smem, smem] + [vmem] * 9,
        out_specs=(vmem,) * (2 + REACH),
        scratch_shapes=[
            pltpu.VMEM((seen, wide), jnp.float32),
            pltpu.VMEM((seen, groups * rows), jnp.bfloat16),
            pltpu.VMEM((seen, groups * rows), jnp.bfloat16),
        ],
        name="attend_grad",
    )(where, doc_lengths, queries, out_grad, keys, values, *far, stats)
    total = own
    for by, part in zip(range(REACH, 0, -1), parts):
        total = total + shifted(part, -by).astype(jnp.float32)
    key_gradient, value_gradient = total.astype(jnp.bfloat16)
    next_rows = jnp.where(
        core == 0, jnp.concatenate([same, other], axis=1), jnp.concatenate([other, same], axis=1)
    )
    return (next_rows[None], query_grad[None], key_gradient[None], value_gradient[None])


def solution(mesh):
    split = P("pipe", "ctx", "dp")
    return jax.shard_map(
        per_device,
        mesh=mesh,
        in_specs=(split, split, split, split, P("pipe", None)),
        out_specs=(P("pipe", ("ctx", "dp"), None), split, split, split),
        check_vma=False,
    )
```
